32 devices in a mesh: dom: 8 (over z, y), sub: 4 (over x, core).
Axes of the slice: x: 2, y: 2, z: 4, core: 2. Of those that a mesh axis runs over, the one named last changes fastest.
Arguments:
- modal_state: float32 [56, 9, 4096], P(None, None, ('dom', 'sub')), may hold values from -6 to 6
- star_mats: float32 [3, 9, 9, 4096], P(None, None, None, ('dom', 'sub')), may hold values from -2 to 2
- face_flux: float32 [2, 4, 9, 9, 4096], P(None, None, None, None, ('dom', 'sub')), may hold values from -1.5 to 1.5
- stiffness: float32 [3, 56, 56], replicated, may hold values from -1 to 1
- stiff_vol: float32 [3, 56, 56], replicated, may hold values from -0.5 to 0.5
- face_proj: float32 [4, 56, 21], replicated, may hold values from -0.75 to 0.75
- face_lifting_matrix: float32 [4, 21, 56], replicated, may hold values from -0.625 to 0.625
- orient_maps: float32 [3, 21, 21], replicated, may hold values from -1.25 to 1.25
- neighbours: int32 [4, 4096], P(None, ('dom', 'sub')), may hold values from -1 to 895, as said below
- face_orient: int32 [4, 4096], P(None, ('dom', 'sub')), may hold values from 0 to 2
- send_slots: int32 [2, 1024], P(None, ('dom', 'sub')), may hold values from 0 to 511
- fast_count: int32 [32], P(('dom', 'sub')), may hold values from 1 to 64, as said below
Outputs:
- new_state: float32 [56, 9, 4096], P(None, None, ('dom', 'sub'))
The draws below stay inside these ranges and needn't reach their ends.
Inputs may be any that keep to these rules, and one draw needn't show every extreme that they name: `neighbours`: entry [j, e] is -1 for an absorbing boundary face; below 512 it names a trace of the element's own device; above, it names a send slot of row 0 of a device of the same partition, or of row 1 of a device one partition lower (offset 4 * 32) or one higher (offset 2 * 4 * 32), as in the reference program; the first and last partitions name no missing side. A device's first fast_count elements form its fast cluster. `send_slots`: entry k of a device's row names the own trace that fills its k-th slot.
All inputs are finite; a program needn't handle non-finite values.
Results may differ from the reference program's by a relative error of at most 0.0003.
Values sent between devices are 32-bit elements; how exact they have to be, the bound alone decides.
A program may use at most 64 MiB of HBM per device.

```python
import math
import jax
import jax.numpy as jnp
from jax import lax

MODES = 56
FIELDS = 9
FACE_MODES = 21
DEGREE = 5
ELEM_DEV = 128
SLOTS_PER_UNIT = 32
FAST_MAX = 64
ELEMS = 4096
SLOTS = 1024
N_DOM = 8
N_SUB = 4


def draw_neighbours(key, part):
    device_count = N_DOM * N_SUB
    elem_total = ELEM_DEV * device_count
    local_len = 4 * ELEM_DEV
    group_len = N_SUB * SLOTS_PER_UNIT
    kind_key, local_key, slot_key = jax.random.split(jax.random.fold_in(key, 11), 3)
    kind_pick = jax.random.randint(kind_key, (4, elem_total), 0, 20)
    local_pick = jax.random.randint(local_key, (4, elem_total), 0, local_len)
    slot_pick = jax.random.randint(slot_key, (4, elem_total), 0, group_len)
    dom_index = jnp.arange(elem_total, dtype=jnp.int32) // ELEM_DEV // N_SUB
    lower_ok = (kind_pick >= 14) & (kind_pick < 17) & (dom_index[None, :] > 0)
    upper_ok = (kind_pick >= 17) & (dom_index[None, :] < N_DOM - 1)
    remote = local_len + slot_pick + jnp.where(lower_ok, group_len, 0) + jnp.where(upper_ok, 2 * group_len, 0)
    values = jnp.where(kind_pick == 0, -1, jnp.where(kind_pick <= 10, local_pick, remote))
    values = values.at[0, 0].set(local_len + 3 * group_len - 1)
    values = values.at[3, elem_total - 1].set(-1)
    return values.astype(jnp.int32)


def draw_fast_count(key, part):
    device_count = N_DOM * N_SUB
    base_key, heavy_key, rank_key = jax.random.split(jax.random.fold_in(key, 23), 3)
    base_load = jax.random.randint(base_key, (device_count,), max(1, FAST_MAX // 8), FAST_MAX // 2 + 1)
    heavy_load = jax.random.randint(heavy_key, (device_count,), 0, 16) == 0
    counts = jnp.where(heavy_load, FAST_MAX, base_load)
    busy_rank = jax.random.randint(rank_key, (), 0, device_count)
    return counts.at[busy_rank].set(FAST_MAX).astype(jnp.int32)


def place_ends(values, key, least, top_value):
    dims = values.shape
    index_at = [jax.random.randint(jax.random.fold_in(key, axis), (), 0, dims[axis]) for axis in range(len(dims))]
    values = values.at[tuple(index_at)].set(least)
    longest = dims.index(max(dims))
    index_at[longest] = (index_at[longest] + 1) % dims[longest]
    return values.at[tuple(index_at)].set(top_value)


def block_scale(rng, dims, cuts, smallest, largest):
    loudness, own = 1.0, jax.random.fold_in(rng, 6)
    for axis_at, parts in cuts:
        heights = jnp.exp(jax.random.uniform(jax.random.fold_in(own, axis_at), (parts,), jnp.float32, smallest / len(cuts), largest / len(cuts)))
        loudness = loudness * jnp.repeat(heights, dims[axis_at] // parts).reshape([-1 if axis == axis_at else 1 for axis in range(len(dims))])
    return loudness


def centred(rng, dims, scale, most, cuts=(), kind=jnp.bfloat16):
    values = scale * jax.random.normal(rng, dims, jnp.float32)
    if cuts:
        values = values * block_scale(rng, dims, cuts, -0.22, 0.18)
    return jnp.clip(values, -most, most).astype(kind)


def setup_inputs(seed: int = 0) -> dict:
    keys = jax.random.split(jax.random.key(seed), 13)
    modal_state = centred(keys[0], (MODES, FIELDS, ELEMS), 1.0, 6.0, ((2, 32),), jnp.float32)
    star_mats = centred(keys[1], (3, FIELDS, FIELDS, ELEMS), FIELDS ** -0.5, 2.0, ((3, 32),), jnp.float32)
    face_flux = centred(keys[2], (2, 4, FIELDS, FIELDS, ELEMS), (2 * FIELDS) ** -0.5, 1.5, ((4, 32),), jnp.float32)
    stiffness = centred(keys[3], (3, MODES, MODES), (3 * MODES // 4) ** -0.5, 1.0, (), jnp.float32)
    stiff_vol = centred(keys[4], (3, MODES, MODES), (3 * MODES) ** -0.5, 0.5, (), jnp.float32)
    face_proj = centred(keys[5], (4, MODES, FACE_MODES), MODES ** -0.5, 0.75, (), jnp.float32)
    face_lifting_matrix = centred(keys[6], (4, FACE_MODES, MODES), (4 * FACE_MODES) ** -0.5, 0.625, (), jnp.float32)
    orient_maps = centred(keys[7], (3, FACE_MODES, FACE_MODES), FACE_MODES ** -0.5, 1.25, (), jnp.float32)
    neighbours = draw_neighbours(jax.random.fold_in(keys[12], 71), 0)
    face_orient = place_ends(jax.random.randint(keys[9], (4, ELEMS), 0, 3), jax.random.fold_in(keys[9], 1), 0, 2).astype(jnp.int32)
    send_slots = place_ends(jax.random.randint(keys[10], (2, SLOTS), 0, 4 * ELEM_DEV), jax.random.fold_in(keys[10], 1), 0, (4 * ELEM_DEV) - 1).astype(jnp.int32)
    fast_count = draw_fast_count(jax.random.fold_in(keys[12], 71), 0)
    return dict(modal_state=modal_state, star_mats=star_mats, face_flux=face_flux, stiffness=stiffness, stiff_vol=stiff_vol, face_proj=face_proj, face_lifting_matrix=face_lifting_matrix, orient_maps=orient_maps, neighbours=neighbours, face_orient=face_orient, send_slots=send_slots, fast_count=fast_count)


half_step = 1.0
highest_derivative_order = lax.Precision.HIGHEST


def time_derivative_terms(state, star_mats, stiffness):
    taylor_terms = [state]
    current = state
    for term_order in range(DEGREE):
        mixed_terms = jnp.einsum('dfge,nge->dnfe', star_mats, current, precision=highest_derivative_order)
        current = -jnp.einsum('dmn,dnfe->mfe', stiffness, mixed_terms, precision=highest_derivative_order)
        taylor_terms.append(current)
    return taylor_terms


def integrate(taylor_terms, start, stop):
    running = jnp.zeros_like(taylor_terms[0])
    for term_order, term_value in enumerate(taylor_terms):
        weight = (stop ** (term_order + 1) - start ** (term_order + 1)) / math.factorial(term_order + 1)
        running = running + weight * term_value
    return running


def project(integral, face_proj):
    return jnp.einsum('jmp,mfe->pfje', face_proj, integral, precision=highest_derivative_order)


def update(integral, own_faces, near_faces, star_mats, face_flux, stiff_vol, face_lifting_matrix):
    mixed_terms = jnp.einsum('dfge,nge->dnfe', star_mats, integral, precision=highest_derivative_order)
    volume = jnp.einsum('dmn,dnfe->mfe', stiff_vol, mixed_terms, precision=highest_derivative_order)
    face_contribution_terms = jnp.einsum('jfge,pgje->pfje', face_flux[0], own_faces, precision=highest_derivative_order)
    face_contribution_terms = face_contribution_terms + jnp.einsum('jfge,pgje->pfje', face_flux[1], near_faces, precision=highest_derivative_order)
    lifted_face_modes = jnp.einsum('dlg,lads->gas', face_lifting_matrix, face_contribution_terms, precision=highest_derivative_order)
    return volume - lifted_face_modes


def resolve(nbr_block, device, send_slots):
    local_len = 4 * ELEM_DEV
    group_len = N_SUB * SLOTS_PER_UNIT
    dom_index = device // N_SUB
    offset = jnp.clip(nbr_block - local_len, 0, 3 * group_len - 1)
    group_id = offset // group_len
    within = offset % group_len
    peer_sub = within // SLOTS_PER_UNIT
    slot_index = within % SLOTS_PER_UNIT
    peer_dom = dom_index + jnp.where(group_id == 1, -1, jnp.where(group_id == 2, 1, 0))
    peer_dev = jnp.clip(peer_dom, 0, N_DOM - 1) * N_SUB + peer_sub
    row_pick = jnp.where(group_id == 0, 0, 1)
    peer_face = send_slots[row_pick, peer_dev * SLOTS_PER_UNIT + slot_index]
    is_local = nbr_block < local_len
    src_dev = jnp.where(is_local, device, peer_dev).astype(jnp.int32)
    src_face = jnp.where(is_local, jnp.maximum(nbr_block, 0), peer_face).astype(jnp.int32)
    return src_dev, src_face, nbr_block >= 0


def reference(modal_state, star_mats, face_flux, stiffness, stiff_vol, face_proj, face_lifting_matrix, orient_maps, neighbours, face_orient, send_slots, fast_count):
    device_count = N_DOM * N_SUB
    elem_count = ELEM_DEV

    def blocks(array):
        lead = array.shape[:-1]
        return jnp.moveaxis(array.reshape(lead + (device_count, elem_count)), -2, 0)

    element_state_full = blocks(modal_state)
    star_all = blocks(star_mats)
    flux_all = blocks(face_flux)
    nbr_all = blocks(neighbours)
    orient_all = blocks(face_orient)
    device_ids = jnp.arange(device_count, dtype=jnp.int32)

    def near_traces(flat_traces, nbr_block, orient_block, device):
        src_dev, src_face, present_element_state = resolve(nbr_block, device, send_slots)
        fetched = flat_traces[src_dev, :, :, src_face]
        fetched = jnp.where(present_element_state[:, :, None, None], fetched, 0.0)
        chosen_maps = orient_maps[orient_block]
        return jnp.einsum('jepq,jeqg->pgje', chosen_maps, fetched, precision=highest_derivative_order)

    def first_pass(inputs):
        state, star_block = inputs
        taylor_terms = time_derivative_terms(state, star_block, stiffness)
        first_part = integrate(taylor_terms, 0.0, half_step)
        second_slow = integrate(taylor_terms, half_step, 2.0 * half_step)
        return first_part, second_slow, project(first_part, face_proj)

    first_all, slow_all, traces_first = lax.map(first_pass, (element_state_full, star_all))
    flat_first = traces_first.reshape(device_count, FACE_MODES, FIELDS, 4 * elem_count)

    def second_pass(inputs):
        device, state, star_block, flux_block, nbr_block, orient_block, first_part, second_slow, own_first = inputs
        near_first = near_traces(flat_first, nbr_block, orient_block, device)
        stepped = state + update(first_part, own_first, near_first, star_block, flux_block, stiff_vol, face_lifting_matrix)
        fast_part = integrate(time_derivative_terms(stepped, star_block, stiffness), 0.0, half_step)
        is_fast = jnp.arange(elem_count, dtype=jnp.int32) < fast_count[device]
        second_part = jnp.where(is_fast, fast_part, second_slow)
        return stepped, second_part, project(second_part, face_proj)

    stepped_all, second_all, traces_second = lax.map(second_pass, (device_ids, element_state_full, star_all, flux_all, nbr_all, orient_all, first_all, slow_all, traces_first))
    flat_second = traces_second.reshape(device_count, FACE_MODES, FIELDS, 4 * elem_count)

    def third_pass(inputs):
        device, stepped, star_block, flux_block, nbr_block, orient_block, second_part, own_second = inputs
        near_second = near_traces(flat_second, nbr_block, orient_block, device)
        return stepped + update(second_part, own_second, near_second, star_block, flux_block, stiff_vol, face_lifting_matrix)

    final_all = lax.map(third_pass, (device_ids, stepped_all, star_all, flux_all, nbr_all, orient_all, second_all, traces_second))
    final_all = jnp.moveaxis(final_all, 0, -2)
    return final_all.reshape(MODES, FIELDS, device_count * elem_count)
```

```python
import functools

import jax
import jax.numpy as jnp
from jax import lax
from jax.experimental import pallas as pl
from jax.experimental.pallas import tpu as pltpu
from jax.sharding import PartitionSpec as P

DEGREE = 5
LANES = 128
F32 = jnp.float32
BF16 = jnp.bfloat16


def up(value, multiple):
    return -(-value // multiple) * multiple


def split(x):
    hi = x.astype(BF16)
    return hi, (x - hi.astype(F32)).astype(BF16)


def stacked(x):
    hi, lo = split(x)
    return jnp.concatenate([hi, lo], axis=0)


def dot(a, b):
    return jnp.dot(a, b, preferred_element_type=F32)


def dot3(w_stack, z_hi, z_lo, rows):
    both = dot(w_stack, z_hi)
    half = w_stack.shape[0] // 2
    return both[:rows] + both[half : half + rows] + dot(w_stack[:half], z_lo)[:rows]


def row_of(ref, *lead_and_row):
    lead, row = lead_and_row[:-1], lead_and_row[-1]
    return ref[(*lead, pl.ds(row, 1), slice(None))]


def kernel(
    sizes,
    state_ref,
    star_ref,
    flux_ref,
    pred_ref,
    proj_ref,
    upd_ref,
    near_idx_ref,
    orient_ref,
    slots_ref,
    count_ref,
    out_ref,
    cur,
    nxt,
    part,
    slow,
    acc,
    trace,
    near,
    remote,
    pred_w,
    proj_w,
    upd_w,
    hot_local,
    hot_remote,
    hot_send,
    mask,
    send,
    recv,
    send_sem,
    recv_sem,
):
    n_dom, n_sub, modes, fields, face_pad, slots = sizes
    width = fields * LANES
    mode_pad = up(modes, 16)
    fold = LANES // slots
    fold_rows = trace.shape[0] // fold
    group = n_sub * slots
    faces = 4
    vol_rows, face_rows = 3 * mode_pad, faces * face_pad
    dom, sub = lax.axis_index("dom"), lax.axis_index("sub")
    has_low, has_high = dom > 0, dom < n_dom - 1

    barrier = pltpu.get_barrier_semaphore()

    def greet(d, s):
        pl.semaphore_signal(
            barrier, inc=1, device_id={"dom": d, "sub": s}, device_id_type=pl.DeviceIdType.MESH
        )

    for k in range(1, n_sub):
        greet(dom, lax.rem(sub + k, n_sub))

    @pl.when(has_low)
    def _():
        for s in range(n_sub):
            greet(dom - 1, s)

    @pl.when(has_high)
    def _():
        for s in range(n_sub):
            greet(dom + 1, s)

    @pl.when(jnp.logical_not(has_low))
    def _():
        recv[:, 1] = jnp.zeros((2, *recv.shape[2:]), F32)

    @pl.when(jnp.logical_not(has_high))
    def _():
        recv[:, 2] = jnp.zeros((2, *recv.shape[2:]), F32)

    pred_w[...] = stacked(pred_ref[...])
    proj_w[...] = stacked(proj_ref[...])
    upd_w[...] = stacked(upd_ref[...])
    trace[fields * face_pad :, :] = jnp.zeros(
        (trace.shape[0] - fields * face_pad, trace.shape[1]), F32
    )
    slow[...] = jnp.zeros_like(slow)
    out_ref[...] = state_ref[...]

    def one_hot(row, rows):
        at = lax.broadcasted_iota(jnp.int32, (rows, LANES), 0)
        return jnp.where(at == row, 1.0, 0.0).astype(BF16)

    own_count = faces * LANES
    for j in range(faces):
        row = near_idx_ref[j : j + 1, :]
        hot_local[:, j * LANES : (j + 1) * LANES] = one_hot(row, own_count)
        hot_remote[:, j * LANES : (j + 1) * LANES] = one_hot(row - own_count, 3 * group)
        turn = orient_ref[j : j + 1, :]
        for o in range(3):
            mask[o, j * face_pad : (j + 1) * face_pad, :] = jnp.broadcast_to(
                jnp.where(turn == o, 1.0, 0.0), (face_pad, LANES)
            )
    for i in range(2):
        hot_send[:, i * LANES : (i + 1) * LANES] = one_hot(slots_ref[i : i + 1, :], own_count)

    def star_rows(src, f):
        high, low = [], []
        for d in range(3):
            for start in range(0, modes, 16):
                count = min(16, modes - start)
                total = None
                for g in range(fields):
                    term = row_of(star_ref, d, f, g) * src[
                        start : start + count, g * LANES : (g + 1) * LANES
                    ]
                    total = term if total is None else total + term
                if count < 16:
                    total = jnp.concatenate([total, jnp.zeros((16 - count, LANES), F32)], axis=0)
                hi, lo = split(total)
                high.append(hi)
                low.append(lo)
        return jnp.concatenate(high, axis=0), jnp.concatenate(low, axis=0)

    def flux_rows(side, src, f):
        blocks = []
        for j in range(faces):
            total = None
            for g in range(fields):
                term = row_of(flux_ref, side, j, f, g) * src[
                    g * face_pad : (g + 1) * face_pad, j * LANES : (j + 1) * LANES
                ]
                total = term if total is None else total + term
            blocks.append(total)
        return split(jnp.concatenate(blocks, axis=0))

    chunks = [tuple(range(f, min(f + 2, fields))) for f in range(0, fields, 2)]

    def side_by_side(pairs):
        return (
            jnp.concatenate([p[0] for p in pairs], axis=1),
            jnp.concatenate([p[1] for p in pairs], axis=1),
        )

    def cols(chunk):
        return slice(chunk[0] * LANES, (chunk[-1] + 1) * LANES)

    def out_copy(ex, which, target, region, lane):
        return pltpu.make_async_remote_copy(
            src_ref=send.at[ex, which],
            dst_ref=recv.at[ex, region, sub],
            send_sem=send_sem.at[ex, region, lane],
            recv_sem=recv_sem.at[ex, region, sub],
            device_id=target,
            device_id_type=pl.DeviceIdType.MESH,
        )

    def exchange_copies(ex):
        inner = [
            out_copy(ex, 0, {"dom": dom, "sub": lax.rem(sub + k, n_sub)}, 0, k)
            for k in range(1, n_sub)
        ]
        lower = [out_copy(ex, 1, {"dom": dom - 1, "sub": s}, 2, s) for s in range(n_sub)]
        upper = [out_copy(ex, 1, {"dom": dom + 1, "sub": s}, 1, s) for s in range(n_sub)]
        return inner, lower, upper

    def arrival(ex, region, s):
        return pltpu.make_async_remote_copy(
            src_ref=send.at[ex, 0],
            dst_ref=recv.at[ex, region, s],
            send_sem=send_sem.at[ex, region, 0],
            recv_sem=recv_sem.at[ex, region, s],
            device_id={"dom": dom, "sub": sub},
            device_id_type=pl.DeviceIdType.MESH,
        )

    peers = n_sub - 1
    is_fast = lax.broadcasted_iota(jnp.int32, (1, LANES), 1) < count_ref[0]

    def stage(ex, carry):
        start = out_ref[...]
        cur[...] = start
        part[...] = start
        acc[...] = start

        def order(k, weights):
            weight, power = weights
            for chunk in chunks:
                hi, lo = side_by_side([star_rows(cur, f) for f in chunk])
                nxt[:, cols(chunk)] = dot3(pred_w[...], hi, lo, modes)
            weight = weight / (k.astype(F32) + 2.0)
            power = power * 2.0
            value = nxt[...]
            cur[...] = value
            part[...] = part[...] + weight * value
            acc[...] = acc[...] + ((power - 1.0) * weight) * value
            return weight, power

        lax.fori_loop(0, DEGREE, order, (jnp.float32(1.0), jnp.float32(2.0)))
        keep = jnp.logical_or(is_fast, ex == 0)
        for g in range(fields):
            at = slice(g * LANES, (g + 1) * LANES)
            part[:, at] = jnp.where(keep, part[:, at], slow[:, at])
        slow[...] = acc[...]

        pad_rows = mode_pad - modes
        for chunk in chunks:
            hi, lo = split(
                jnp.concatenate(
                    [part[:, cols(chunk)], jnp.zeros((pad_rows, len(chunk) * LANES), F32)], axis=0
                )
            )
            value = dot3(proj_w[...], hi, lo, face_rows)
            for i, g in enumerate(chunk):
                for j in range(faces):
                    trace[g * face_pad : (g + 1) * face_pad, j * LANES : (j + 1) * LANES] = value[
                        j * face_pad : (j + 1) * face_pad, i * LANES : (i + 1) * LANES
                    ]

        table = stacked(trace[...])
        rows = trace.shape[0]
        picked = dot(table, hot_send[...])
        picked = picked[:rows] + picked[rows:]
        section = lax.broadcasted_iota(jnp.int32, (fold_rows, LANES), 1) // slots
        for i in range(2):
            lanes = slice(i * LANES, (i + 1) * LANES)
            packed = picked[:fold_rows, lanes]
            for a in range(1, fold):
                packed = jnp.where(
                    section == a, picked[a * fold_rows : (a + 1) * fold_rows, lanes], packed
                )
            send[ex, i] = packed
            if i == 0:
                recv[ex, 0, sub] = packed

        @pl.when(ex == 0)
        def _():
            pl.semaphore_wait(
                barrier, peers + n_sub * has_low.astype(jnp.int32) + n_sub * has_high.astype(jnp.int32)
            )

        inner, lower, upper = exchange_copies(ex)

        @pl.when(has_low)
        def _():
            for copy in lower:
                copy.start()

        @pl.when(has_high)
        def _():
            for copy in upper:
                copy.start()

        for copy in inner:
            copy.start()

        found = dot(table, hot_local[...])
        near[...] = found[:rows] + found[rows:]
        base = vol_rows + face_rows
        for chunk in chunks:
            pairs = []
            for f in chunk:
                vol, own = star_rows(part, f), flux_rows(0, trace, f)
                pairs.append([jnp.concatenate([vol[i], own[i]], axis=0) for i in range(2)])
            hi, lo = side_by_side(pairs)
            out_ref[:, cols(chunk)] += dot3(upd_w[:, :base], hi, lo, modes)

        for k in range(1, n_sub):
            arrival(ex, 0, lax.rem(sub + k, n_sub)).wait_recv()

        @pl.when(has_low)
        def _():
            for s in range(n_sub):
                arrival(ex, 1, s).wait_recv()

        @pl.when(has_high)
        def _():
            for s in range(n_sub):
                arrival(ex, 2, s).wait_recv()

        for region in range(3):
            for b in range(n_sub // fold):
                blocks = [recv[ex, region, b * fold + i] for i in range(fold)]
                for a in range(fold):
                    value = None
                    for i in range(fold):
                        moved = blocks[i]
                        if i != a:
                            moved = pltpu.roll(moved, ((i - a) * slots) % LANES, 1)
                        value = moved if value is None else jnp.where(section == i, moved, value)
                    first = region * group + b * LANES
                    remote[a * fold_rows : (a + 1) * fold_rows, first : first + LANES] = value
        found = dot(stacked(remote[...]), hot_remote[...])
        near[...] = near[...] + found[:rows] + found[rows:]

        masks = [mask[o].astype(BF16) for o in range(3)]
        for chunk in chunks:
            pairs = []
            for f in chunk:
                hi, lo = flux_rows(1, near, f)
                pairs.append(
                    [
                        jnp.concatenate([value * masks[o] for o in range(3)], axis=0)
                        for value in (hi, lo)
                    ]
                )
            hi, lo = side_by_side(pairs)
            out_ref[:, cols(chunk)] += dot3(upd_w[:, base:], hi, lo, modes)

        for copy in inner:
            copy.wait_send()

        @pl.when(has_low)
        def _():
            for copy in lower:
                copy.wait_send()

        @pl.when(has_high)
        def _():
            for copy in upper:
                copy.wait_send()

        return carry

    lax.fori_loop(0, 2, stage, 0)


def padded(x, *shape):
    return jnp.pad(x, [(0, want - have) for want, have in zip(shape, x.shape)])


def local(
    n_dom,
    n_sub,
    modal_state,
    star_mats,
    face_flux,
    stiffness,
    stiff_vol,
    face_proj,
    face_lifting_matrix,
    orient_maps,
    neighbours,
    face_orient,
    send_slots,
    fast_count,
):
    modes, fields, elems = modal_state.shape
    face_modes = orient_maps.shape[1]
    slots = send_slots.shape[1]
    fold = LANES // slots
    face_pad, mode_pad = up(face_modes, 8), up(modes, 16)
    table_rows = up(fields * face_pad, 8 * fold)
    group = n_sub * slots
    width = fields * elems
    exact = lax.Precision.HIGHEST

    def wide(mats):
        mats = padded(mats, 3, mode_pad, mode_pad)
        return mats.transpose(1, 0, 2).reshape(mode_pad, -1)

    lift = padded(face_lifting_matrix, 4, face_pad, mode_pad)
    turned = jnp.einsum("jpm,opq->mojq", lift, padded(orient_maps, 3, face_pad, face_pad), precision=exact)
    pred = -wide(stiffness)
    proj = padded(face_proj, 4, mode_pad, face_pad).transpose(0, 2, 1).reshape(-1, mode_pad)
    upd = jnp.concatenate(
        [
            wide(stiff_vol),
            -lift.transpose(2, 0, 1).reshape(mode_pad, -1),
            -turned.reshape(mode_pad, -1),
        ],
        axis=1,
    )
    upd_cols = upd.shape[1]
    vmem = pl.BlockSpec(memory_space=pltpu.VMEM)
    out = pl.pallas_call(
        functools.partial(kernel, (n_dom, n_sub, modes, fields, face_pad, slots)),
        out_shape=jax.ShapeDtypeStruct((modes, width), F32),
        in_specs=[vmem] * 9 + [pl.BlockSpec(memory_space=pltpu.SMEM)],
        out_specs=vmem,
        scratch_shapes=[
            pltpu.VMEM((modes, width), F32),
            pltpu.VMEM((modes, width), F32),
            pltpu.VMEM((modes, width), F32),
            pltpu.VMEM((modes, width), F32),
            pltpu.VMEM((modes, width), F32),
            pltpu.VMEM((table_rows, 4 * elems), F32),
            pltpu.VMEM((table_rows, 4 * elems), F32),
            pltpu.VMEM((table_rows, 3 * group), F32),
            pltpu.VMEM((2 * mode_pad, 3 * mode_pad), BF16),
            pltpu.VMEM((8 * face_pad, mode_pad), BF16),
            pltpu.VMEM((2 * mode_pad, upd_cols), BF16),
            pltpu.VMEM((4 * elems, 4 * elems), BF16),
            pltpu.VMEM((3 * group, 4 * elems), BF16),
            pltpu.VMEM((4 * elems, 2 * LANES), BF16),
            pltpu.VMEM((3, 4 * face_pad, LANES), F32),
            pltpu.VMEM((2, 2, table_rows // fold, LANES), F32),
            pltpu.VMEM((2, 3, n_sub, table_rows // fold, LANES), F32),
            pltpu.SemaphoreType.DMA((2, 3, n_sub)),
            pltpu.SemaphoreType.DMA((2, 3, n_sub)),
        ],
        compiler_params=pltpu.CompilerParams(collective_id=0, has_side_effects=True),
    )(
        modal_state.reshape(modes, width),
        star_mats,
        face_flux,
        pred,
        proj,
        upd,
        neighbours,
        face_orient,
        jnp.tile(send_slots, (1, fold)),
        fast_count,
    )
    return out.reshape(modes, fields, elems)


def solution(mesh):
    split_last = ("dom", "sub")
    placed = (
        P(None, None, split_last),
        P(None, None, None, split_last),
        P(None, None, None, None, split_last),
        P(),
        P(),
        P(),
        P(),
        P(),
        P(None, split_last),
        P(None, split_last),
        P(None, split_last),
        P(split_last),
    )
    return jax.shard_map(
        functools.partial(local, mesh.shape["dom"], mesh.shape["sub"]),
        mesh=mesh,
        in_specs=placed,
        out_specs=P(None, None, split_last),
        check_vma=False,
    )
```

```python
import functools

import jax
import jax.numpy as jnp
from jax import lax
from jax.experimental import pallas as pl
from jax.experimental.pallas import tpu as pltpu
from jax.sharding import PartitionSpec as P

DEGREE = 5
LANES = 128
F32 = jnp.float32
BF16 = jnp.bfloat16


def up(value, multiple):
    return -(-value // multiple) * multiple


def split(x):
    hi = x.astype(BF16)
    return hi, (x - hi.astype(F32)).astype(BF16)


def stacked(x):
    hi, lo = split(x)
    return jnp.concatenate([hi, lo], axis=0)


def dot(a, b):
    return jnp.dot(a, b, preferred_element_type=F32)


def dot3(w_stack, z_hi, z_lo, rows):
    both = dot(w_stack, z_hi)
    half = w_stack.shape[0] // 2
    return both[:rows] + both[half : half + rows] + dot(w_stack[:half], z_lo)[:rows]


def grow8(x):
    return jnp.concatenate([x, jnp.zeros((8 - x.shape[0], x.shape[1]), F32)], axis=0)


def row_of(ref, *lead_and_row):
    lead, row = lead_and_row[:-1], lead_and_row[-1]
    return ref[(*lead, pl.ds(row, 1), slice(None))]


def kernel(
    sizes,
    state_hbm,
    star_hbm,
    flux_hbm,
    stiff_hbm,
    vol_hbm,
    proj_hbm,
    lift_hbm,
    maps_hbm,
    near_idx_ref,
    orient_ref,
    slots_ref,
    count_ref,
    out_ref,
    star_ref,
    flux_ref,
    stiff_ref,
    vol_ref,
    proj_ref,
    lift_ref,
    maps_ref,
    load_sem,
    cur,
    nxt,
    part,
    slow,
    acc,
    trace,
    near,
    remote,
    pred_w,
    proj_w,
    upd_w,
    hot_local,
    hot_remote,
    hot_send,
    mask,
    send,
    recv,
    send_sem,
    recv_sem,
):
    n_dom, n_sub, modes, fields, face_pad, slots = sizes
    width = fields * LANES
    mode_pad = up(modes, 16)
    fold = LANES // slots
    fold_rows = trace.shape[0] // fold
    group = n_sub * slots
    faces = 4
    vol_rows, face_rows = 3 * mode_pad, faces * face_pad
    loads = [
        pltpu.make_async_copy(source, target, load_sem.at[i])
        for i, (source, target) in enumerate(
            [
                (stiff_hbm, stiff_ref),
                (vol_hbm, vol_ref),
                (proj_hbm, proj_ref),
                (lift_hbm, lift_ref),
                (maps_hbm, maps_ref),
                (state_hbm, out_ref),
                (star_hbm, star_ref),
                (flux_hbm, flux_ref),
            ]
        )
    ]
    for load in loads:
        load.start()
    dom, sub = lax.axis_index("dom"), lax.axis_index("sub")
    has_low, has_high = dom > 0, dom < n_dom - 1

    barrier = pltpu.get_barrier_semaphore()

    def greet(d, s):
        pl.semaphore_signal(
            barrier, inc=1, device_id={"dom": d, "sub": s}, device_id_type=pl.DeviceIdType.MESH
        )

    for k in range(1, n_sub):
        greet(dom, lax.rem(sub + k, n_sub))

    @pl.when(has_low)
    def _():
        for s in range(n_sub):
            greet(dom - 1, s)

    @pl.when(has_high)
    def _():
        for s in range(n_sub):
            greet(dom + 1, s)

    @pl.when(jnp.logical_not(has_low))
    def _():
        recv[:, 1] = jnp.zeros((2, *recv.shape[2:]), F32)

    @pl.when(jnp.logical_not(has_high))
    def _():
        recv[:, 2] = jnp.zeros((2, *recv.shape[2:]), F32)

    trace[fields * face_pad :, :] = jnp.zeros(
        (trace.shape[0] - fields * face_pad, trace.shape[1]), F32
    )
    slow[...] = jnp.zeros_like(slow)

    def one_hot(row, rows):
        at = lax.broadcasted_iota(jnp.int32, (rows, LANES), 0)
        return jnp.where(at == row, 1.0, 0.0).astype(BF16)

    own_count = faces * LANES
    for j in range(faces):
        row = near_idx_ref[j : j + 1, :]
        hot_local[:, j * LANES : (j + 1) * LANES] = one_hot(row, own_count)
        hot_remote[:, j * LANES : (j + 1) * LANES] = one_hot(row - own_count, 3 * group)
        turn = orient_ref[j : j + 1, :]
        for o in range(3):
            mask[o, j * face_pad : (j + 1) * face_pad, :] = jnp.broadcast_to(
                jnp.where(turn == o, 1.0, 0.0), (face_pad, LANES)
            )

    def at_columns(rows, columns, test):
        row = lax.broadcasted_iota(jnp.int32, (rows, columns), 0)
        column = lax.broadcasted_iota(jnp.int32, (rows, columns), 1)
        return jnp.where(test(row, column), 1.0, 0.0).astype(BF16)

    tiled = dot(
        stacked(grow8(slots_ref[...].astype(F32))),
        at_columns(slots, LANES, lambda row, column: column % slots == row),
    )
    tiled = (tiled[:8] + tiled[8:]).astype(jnp.int32)
    for i in range(2):
        hot_send[:, i * LANES : (i + 1) * LANES] = one_hot(tiled[i : i + 1, :], own_count)

    for load in loads[:5]:
        load.wait()

    def grow(x, rows):
        return jnp.concatenate([x, jnp.zeros((rows - x.shape[0], x.shape[1]), F32)], axis=0)

    def shifted(rows, columns, shift):
        return at_columns(rows, columns, lambda row, column: column == row + shift)

    def spread(ref):
        value = None
        for d in range(3):
            term = dot(stacked(grow(ref[d], mode_pad)), shifted(modes, vol_rows, d * mode_pad))
            value = term if value is None else value + term
        return value

    face_modes = maps_ref.shape[1]
    pred_w[...] = (-spread(stiff_ref)).astype(BF16)
    upd_w[:, :vol_rows] = spread(vol_ref).astype(BF16)

    def by_face(ref):
        return jnp.concatenate([grow(ref[:, j, :], face_pad) for j in range(faces)], axis=0)

    proj_w[...] = stacked(by_face(proj_ref))
    same = shifted(mode_pad, modes, 0)
    turn_lift = []
    for value in split(-by_face(lift_ref)):
        turn_lift.append(
            lax.dot_general(same, value, (((1,), (1,)), ((), ())), preferred_element_type=F32)
        )
    turn_lift = jnp.concatenate(turn_lift, axis=0).astype(BF16)
    upd_w[:, vol_rows : vol_rows + face_rows] = turn_lift
    turned = None
    for o in range(3):
        place = at_columns(
            face_modes,
            3 * face_rows,
            lambda row, column: (column // face_rows == o) & (column % face_pad == row),
        )
        both = dot(stacked(grow(maps_ref[o], up(face_pad, 16))), place)
        term = both[:face_pad] + both[up(face_pad, 16) :][:face_pad]
        turned = term if turned is None else turned + term
    turned = jnp.concatenate([turned] * faces, axis=0)
    row = lax.broadcasted_iota(jnp.int32, turned.shape, 0)
    column = lax.broadcasted_iota(jnp.int32, turned.shape, 1)
    turned = jnp.where(column % face_rows // face_pad == row // face_pad, turned, 0.0)
    upd_w[:, vol_rows + face_rows :] = stacked(dot3(turn_lift, *split(turned), mode_pad))
    for load in loads[5:]:
        load.wait()

    def star_rows(src, f):
        high, low = [], []
        for d in range(3):
            for start in range(0, modes, 16):
                count = min(16, modes - start)
                total = None
                for g in range(fields):
                    term = row_of(star_ref, f, g, d) * src[
                        start : start + count, g * LANES : (g + 1) * LANES
                    ]
                    total = term if total is None else total + term
                if count < 16:
                    total = jnp.concatenate([total, jnp.zeros((16 - count, LANES), F32)], axis=0)
                hi, lo = split(total)
                high.append(hi)
                low.append(lo)
        return jnp.concatenate(high, axis=0), jnp.concatenate(low, axis=0)

    def flux_rows(side, src, f):
        blocks = []
        for j in range(faces):
            total = None
            for g in range(fields):
                term = row_of(flux_ref, side, f, g, j) * src[
                    g * face_pad : (g + 1) * face_pad, j * LANES : (j + 1) * LANES
                ]
                total = term if total is None else total + term
            blocks.append(total)
        return split(jnp.concatenate(blocks, axis=0))

    chunks = [tuple(range(f, min(f + 2, fields))) for f in range(0, fields, 2)]

    def add_out(chunk, value):
        for i, f in enumerate(chunk):
            out_ref[f] = out_ref[f] + value[:, i * LANES : (i + 1) * LANES]

    def side_by_side(pairs):
        return (
            jnp.concatenate([p[0] for p in pairs], axis=1),
            jnp.concatenate([p[1] for p in pairs], axis=1),
        )

    def cols(chunk):
        return slice(chunk[0] * LANES, (chunk[-1] + 1) * LANES)

    def out_copy(ex, which, target, region, lane):
        return pltpu.make_async_remote_copy(
            src_ref=send.at[ex, which],
            dst_ref=recv.at[ex, region, sub],
            send_sem=send_sem.at[ex, region, lane],
            recv_sem=recv_sem.at[ex, region, sub],
            device_id=target,
            device_id_type=pl.DeviceIdType.MESH,
        )

    def exchange_copies(ex):
        inner = [
            out_copy(ex, 0, {"dom": dom, "sub": lax.rem(sub + k, n_sub)}, 0, k)
            for k in range(1, n_sub)
        ]
        lower = [out_copy(ex, 1, {"dom": dom - 1, "sub": s}, 2, s) for s in range(n_sub)]
        upper = [out_copy(ex, 1, {"dom": dom + 1, "sub": s}, 1, s) for s in range(n_sub)]
        return inner, lower, upper

    def arrival(ex, region, s):
        return pltpu.make_async_remote_copy(
            src_ref=send.at[ex, 0],
            dst_ref=recv.at[ex, region, s],
            send_sem=send_sem.at[ex, region, 0],
            recv_sem=recv_sem.at[ex, region, s],
            device_id={"dom": dom, "sub": sub},
            device_id_type=pl.DeviceIdType.MESH,
        )

    peers = n_sub - 1
    is_fast = lax.broadcasted_iota(jnp.int32, (1, LANES), 1) < count_ref[0]

    def stage(ex, carry):
        for f in range(fields):
            at = slice(f * LANES, (f + 1) * LANES)
            start = out_ref[f]
            cur[:, at] = start
            part[:, at] = start
            acc[:, at] = start

        def order(k, weights):
            weight, power = weights
            for chunk in chunks:
                hi, lo = side_by_side([star_rows(cur, f) for f in chunk])
                nxt[:, cols(chunk)] = dot3(pred_w[...], hi, lo, modes)
            weight = weight / (k.astype(F32) + 2.0)
            power = power * 2.0
            value = nxt[...]
            cur[...] = value
            part[...] = part[...] + weight * value
            acc[...] = acc[...] + ((power - 1.0) * weight) * value
            return weight, power

        lax.fori_loop(0, DEGREE, order, (jnp.float32(1.0), jnp.float32(2.0)))
        keep = jnp.logical_or(is_fast, ex == 0)
        for g in range(fields):
            at = slice(g * LANES, (g + 1) * LANES)
            part[:, at] = jnp.where(keep, part[:, at], slow[:, at])
        slow[...] = acc[...]

        for chunk in chunks:
            hi, lo = split(part[:, cols(chunk)])
            value = dot3(proj_w[...], hi, lo, face_rows)
            for i, g in enumerate(chunk):
                for j in range(faces):
                    trace[g * face_pad : (g + 1) * face_pad, j * LANES : (j + 1) * LANES] = value[
                        j * face_pad : (j + 1) * face_pad, i * LANES : (i + 1) * LANES
                    ]

        table = stacked(trace[...])
        rows = trace.shape[0]
        picked = dot(table, hot_send[...])
        picked = picked[:rows] + picked[rows:]
        section = lax.broadcasted_iota(jnp.int32, (fold_rows, LANES), 1) // slots
        for i in range(2):
            lanes = slice(i * LANES, (i + 1) * LANES)
            packed = picked[:fold_rows, lanes]
            for a in range(1, fold):
                packed = jnp.where(
                    section == a, picked[a * fold_rows : (a + 1) * fold_rows, lanes], packed
                )
            send[ex, i] = packed
            if i == 0:
                recv[ex, 0, sub] = packed

        @pl.when(ex == 0)
        def _():
            pl.semaphore_wait(
                barrier, peers + n_sub * has_low.astype(jnp.int32) + n_sub * has_high.astype(jnp.int32)
            )

        inner, lower, upper = exchange_copies(ex)

        @pl.when(has_low)
        def _():
            for copy in lower:
                copy.start()

        @pl.when(has_high)
        def _():
            for copy in upper:
                copy.start()

        for copy in inner:
            copy.start()

        found = dot(table, hot_local[...])
        near[...] = found[:rows] + found[rows:]
        base = vol_rows + face_rows
        for chunk in chunks:
            pairs = []
            for f in chunk:
                vol, own = star_rows(part, f), flux_rows(0, trace, f)
                pairs.append([jnp.concatenate([vol[i], own[i]], axis=0) for i in range(2)])
            hi, lo = side_by_side(pairs)
            add_out(chunk, dot3(upd_w[:, :base], hi, lo, modes))

        for k in range(1, n_sub):
            arrival(ex, 0, lax.rem(sub + k, n_sub)).wait_recv()

        @pl.when(has_low)
        def _():
            for s in range(n_sub):
                arrival(ex, 1, s).wait_recv()

        @pl.when(has_high)
        def _():
            for s in range(n_sub):
                arrival(ex, 2, s).wait_recv()

        for region in range(3):
            for b in range(n_sub // fold):
                blocks = [recv[ex, region, b * fold + i] for i in range(fold)]
                for a in range(fold):
                    value = None
                    for i in range(fold):
                        moved = blocks[i]
                        if i != a:
                            moved = pltpu.roll(moved, ((i - a) * slots) % LANES, 1)
                        value = moved if value is None else jnp.where(section == i, moved, value)
                    first = region * group + b * LANES
                    remote[a * fold_rows : (a + 1) * fold_rows, first : first + LANES] = value
        found = dot(stacked(remote[...]), hot_remote[...])
        near[...] = near[...] + found[:rows] + found[rows:]

        masks = [mask[o].astype(BF16) for o in range(3)]
        for chunk in chunks:
            pairs = []
            for f in chunk:
                hi, lo = flux_rows(1, near, f)
                pairs.append(
                    [
                        jnp.concatenate([value * masks[o] for o in range(3)], axis=0)
                        for value in (hi, lo)
                    ]
                )
            hi, lo = side_by_side(pairs)
            add_out(chunk, dot3(upd_w[:, base:], hi, lo, modes))

        for copy in inner:
            copy.wait_send()

        @pl.when(has_low)
        def _():
            for copy in lower:
                copy.wait_send()

        @pl.when(has_high)
        def _():
            for copy in upper:
                copy.wait_send()

        return carry

    lax.fori_loop(0, 2, stage, 0)


def local(
    n_dom,
    n_sub,
    modal_state,
    star_mats,
    face_flux,
    stiffness,
    stiff_vol,
    face_proj,
    face_lifting_matrix,
    orient_maps,
    neighbours,
    face_orient,
    send_slots,
    fast_count,
):
    modes, fields, elems = modal_state.shape
    face_modes = orient_maps.shape[1]
    slots = send_slots.shape[1]
    fold = LANES // slots
    face_pad, mode_pad = up(face_modes, 8), up(modes, 16)
    table_rows = up(fields * face_pad, 8 * fold)
    group = n_sub * slots
    width = fields * elems
    upd_cols = 3 * mode_pad + 4 * 4 * face_pad
    any_space = pl.BlockSpec(memory_space=pl.ANY)
    vmem = pl.BlockSpec(memory_space=pltpu.VMEM)
    out = pl.pallas_call(
        functools.partial(kernel, (n_dom, n_sub, modes, fields, face_pad, slots)),
        out_shape=jax.ShapeDtypeStruct((fields, modes, elems), F32),
        in_specs=[any_space] * 8 + [vmem] * 3 + [pl.BlockSpec(memory_space=pltpu.SMEM)],
        out_specs=vmem,
        scratch_shapes=[
            pltpu.VMEM((fields, fields, 3, elems), F32),
            pltpu.VMEM((2, fields, fields, 4, elems), F32),
            pltpu.VMEM((3, modes, modes), F32),
            pltpu.VMEM((3, modes, modes), F32),
            pltpu.VMEM((face_modes, 4, modes), F32),
            pltpu.VMEM((face_modes, 4, modes), F32),
            pltpu.VMEM((3, face_modes, face_modes), F32),
            pltpu.SemaphoreType.DMA((8,)),
            pltpu.VMEM((modes, width), F32),
            pltpu.VMEM((modes, width), F32),
            pltpu.VMEM((modes, width), F32),
            pltpu.VMEM((modes, width), F32),
            pltpu.VMEM((modes, width), F32),
            pltpu.VMEM((table_rows, 4 * elems), F32),
            pltpu.VMEM((table_rows, 4 * elems), F32),
            pltpu.VMEM((table_rows, 3 * group), F32),
            pltpu.VMEM((2 * mode_pad, 3 * mode_pad), BF16),
            pltpu.VMEM((8 * face_pad, modes), BF16),
            pltpu.VMEM((2 * mode_pad, upd_cols), BF16),
            pltpu.VMEM((4 * elems, 4 * elems), BF16),
            pltpu.VMEM((3 * group, 4 * elems), BF16),
            pltpu.VMEM((4 * elems, 2 * LANES), BF16),
            pltpu.VMEM((3, 4 * face_pad, LANES), F32),
            pltpu.VMEM((2, 2, table_rows // fold, LANES), F32),
            pltpu.VMEM((2, 3, n_sub, table_rows // fold, LANES), F32),
            pltpu.SemaphoreType.DMA((2, 3, n_sub)),
            pltpu.SemaphoreType.DMA((2, 3, n_sub)),
        ],
        compiler_params=pltpu.CompilerParams(collective_id=0, has_side_effects=True),
    )(
        modal_state.transpose(1, 0, 2),
        star_mats.transpose(1, 2, 0, 3),
        face_flux.transpose(0, 2, 3, 1, 4),
        stiffness,
        stiff_vol,
        face_proj.transpose(2, 0, 1),
        face_lifting_matrix.transpose(1, 0, 2),
        orient_maps,
        neighbours,
        face_orient,
        send_slots,
        fast_count,
    )
    return out.transpose(1, 0, 2)


def solution(mesh):
    split_last = ("dom", "sub")
    placed = (
        P(None, None, split_last),
        P(None, None, None, split_last),
        P(None, None, None, None, split_last),
        P(),
        P(),
        P(),
        P(),
        P(),
        P(None, split_last),
        P(None, split_last),
        P(None, split_last),
        P(split_last),
    )
    return jax.shard_map(
        functools.partial(local, mesh.shape["dom"], mesh.shape["sub"]),
        mesh=mesh,
        in_specs=placed,
        out_specs=P(None, None, split_last),
        check_vma=False,
    )
```

```python
import functools

import jax
import jax.numpy as jnp
from jax import lax
from jax.experimental import pallas as pl
from jax.experimental.pallas import tpu as pltpu
from jax.sharding import PartitionSpec as P

DEGREE = 5
LANES = 128
F32 = jnp.float32
BF16 = jnp.bfloat16


def up(value, multiple):
    return -(-value // multiple) * multiple


def split(x):
    hi = x.astype(BF16)
    return hi, (x - hi.astype(F32)).astype(BF16)


def stacked(x):
    hi, lo = split(x)
    return jnp.concatenate([hi, lo], axis=0)


def dot(a, b):
    return jnp.dot(a, b, preferred_element_type=F32)


def dot3(w_stack, z_hi, z_lo, rows):
    both = dot(w_stack, z_hi)
    half = w_stack.shape[0] // 2
    return both[:rows] + both[half : half + rows] + dot(w_stack[:half], z_lo)[:rows]


def grow8(x):
    return jnp.concatenate([x, jnp.zeros((8 - x.shape[0], x.shape[1]), F32)], axis=0)


def row_of(ref, *lead_and_row):
    lead, row = lead_and_row[:-1], lead_and_row[-1]
    return ref[(*lead, pl.ds(row, 1), slice(None))]


def kernel(
    sizes,
    state_hbm,
    star_hbm,
    flux_hbm,
    stiff_hbm,
    vol_hbm,
    proj_hbm,
    lift_hbm,
    maps_hbm,
    near_idx_ref,
    orient_ref,
    slots_ref,
    count_ref,
    out_ref,
    star_ref,
    flux_ref,
    stiff_ref,
    vol_ref,
    proj_ref,
    lift_ref,
    maps_ref,
    load_sem,
    cur,
    nxt,
    part,
    slow,
    acc,
    trace,
    near,
    remote,
    pred_w,
    proj_w,
    upd_w,
    hot_local,
    hot_remote,
    hot_send,
    mask,
    send,
    recv,
    send_sem,
    recv_sem,
    forward_sem,
):
    n_dom, n_sub, modes, fields, face_pad, slots = sizes
    width = fields * LANES
    mode_pad = up(modes, 16)
    fold = LANES // slots
    fold_rows = trace.shape[0] // fold
    group = n_sub * slots
    faces = 4
    vol_rows, face_rows = 3 * mode_pad, faces * face_pad
    loads = [
        pltpu.make_async_copy(source, target, load_sem.at[i])
        for i, (source, target) in enumerate(
            [
                (stiff_hbm, stiff_ref),
                (vol_hbm, vol_ref),
                (proj_hbm, proj_ref),
                (lift_hbm, lift_ref),
                (maps_hbm, maps_ref),
                (state_hbm, out_ref),
                (star_hbm, star_ref),
                (flux_hbm, flux_ref),
            ]
        )
    ]
    for load in loads:
        load.start()
    dom, sub = lax.axis_index("dom"), lax.axis_index("sub")
    has_low, has_high = dom > 0, dom < n_dom - 1

    barrier = pltpu.get_barrier_semaphore()

    def greet(d, s):
        pl.semaphore_signal(
            barrier, inc=1, device_id={"dom": d, "sub": s}, device_id_type=pl.DeviceIdType.MESH
        )

    chips = n_sub // 2
    chip, core = sub // 2, lax.rem(sub, 2)
    sibling = 2 * chip + 1 - core

    greet(dom, sibling)
    for k in range(1, chips):
        greet(dom, 2 * lax.rem(chip + k, chips) + core)

    @pl.when(has_low)
    def _():
        for c in range(chips):
            greet(dom - 1, 2 * c + core)

    @pl.when(has_high)
    def _():
        for c in range(chips):
            greet(dom + 1, 2 * c + core)

    @pl.when(jnp.logical_not(has_low))
    def _():
        recv[:, 1] = jnp.zeros((2, *recv.shape[2:]), F32)

    @pl.when(jnp.logical_not(has_high))
    def _():
        recv[:, 2] = jnp.zeros((2, *recv.shape[2:]), F32)

    trace[fields * face_pad :, :] = jnp.zeros(
        (trace.shape[0] - fields * face_pad, trace.shape[1]), F32
    )
    slow[...] = jnp.zeros_like(slow)

    def one_hot(row, rows):
        at = lax.broadcasted_iota(jnp.int32, (rows, LANES), 0)
        return jnp.where(at == row, 1.0, 0.0).astype(BF16)

    own_count = faces * LANES
    def at_columns(rows, columns, test):
        row = lax.broadcasted_iota(jnp.int32, (rows, columns), 0)
        column = lax.broadcasted_iota(jnp.int32, (rows, columns), 1)
        return jnp.where(test(row, column), 1.0, 0.0).astype(BF16)

    tiled = dot(
        stacked(grow8(slots_ref[...].astype(F32))),
        at_columns(slots, LANES, lambda row, column: column % slots == row),
    )
    tiled = (tiled[:8] + tiled[8:]).astype(jnp.int32)
    for i in range(2):
        hot_send[:, i * LANES : (i + 1) * LANES] = one_hot(tiled[i : i + 1, :], own_count)

    for load in loads[:5]:
        load.wait()

    def grow(x, rows):
        return jnp.concatenate([x, jnp.zeros((rows - x.shape[0], x.shape[1]), F32)], axis=0)

    def shifted(rows, columns, shift):
        return at_columns(rows, columns, lambda row, column: column == row + shift)

    def spread(ref):
        value = None
        for d in range(3):
            term = dot(stacked(grow(ref[d], mode_pad)), shifted(modes, vol_rows, d * mode_pad))
            value = term if value is None else value + term
        return value

    face_modes = maps_ref.shape[1]
    pred_w[...] = (-spread(stiff_ref)).astype(BF16)
    def by_face(ref):
        return jnp.concatenate([grow(ref[:, j, :], face_pad) for j in range(faces)], axis=0)

    proj_w[...] = stacked(by_face(proj_ref))
    def prepare_update():
        for j in range(faces):
            row = near_idx_ref[j : j + 1, :]
            hot_local[:, j * LANES : (j + 1) * LANES] = one_hot(row, own_count)
            hot_remote[:, j * LANES : (j + 1) * LANES] = one_hot(row - own_count, 3 * group)
            turn = orient_ref[j : j + 1, :]
            for o in range(3):
                mask[o, j * face_pad : (j + 1) * face_pad, :] = jnp.broadcast_to(
                    jnp.where(turn == o, 1.0, 0.0), (face_pad, LANES)
                )
        upd_w[:, :vol_rows] = spread(vol_ref).astype(BF16)
        same = shifted(mode_pad, modes, 0)
        turn_lift = []
        for value in split(-by_face(lift_ref)):
            turn_lift.append(
                lax.dot_general(same, value, (((1,), (1,)), ((), ())), preferred_element_type=F32)
            )
        turn_lift = jnp.concatenate(turn_lift, axis=0).astype(BF16)
        upd_w[:, vol_rows : vol_rows + face_rows] = turn_lift
        turned = None
        for o in range(3):
            place = at_columns(
                face_modes,
                3 * face_rows,
                lambda row, column: (column // face_rows == o) & (column % face_pad == row),
            )
            both = dot(stacked(grow(maps_ref[o], up(face_pad, 16))), place)
            term = both[:face_pad] + both[up(face_pad, 16) :][:face_pad]
            turned = term if turned is None else turned + term
        turned = jnp.concatenate([turned] * faces, axis=0)
        row = lax.broadcasted_iota(jnp.int32, turned.shape, 0)
        column = lax.broadcasted_iota(jnp.int32, turned.shape, 1)
        turned = jnp.where(column % face_rows // face_pad == row // face_pad, turned, 0.0)
        upd_w[:, vol_rows + face_rows :] = stacked(dot3(turn_lift, *split(turned), mode_pad))

    for load in loads[5:]:
        load.wait()

    def star_rows(src, f):
        high, low = [], []
        for d in range(3):
            for start in range(0, modes, 16):
                count = min(16, modes - start)
                total = None
                for g in range(fields):
                    term = row_of(star_ref, f, g, d) * src[
                        start : start + count, g * LANES : (g + 1) * LANES
                    ]
                    total = term if total is None else total + term
                if count < 16:
                    total = jnp.concatenate([total, jnp.zeros((16 - count, LANES), F32)], axis=0)
                hi, lo = split(total)
                high.append(hi)
                low.append(lo)
        return jnp.concatenate(high, axis=0), jnp.concatenate(low, axis=0)

    def flux_rows(side, src, f):
        blocks = []
        for j in range(faces):
            total = None
            for g in range(fields):
                term = row_of(flux_ref, side, f, g, j) * src[
                    g * face_pad : (g + 1) * face_pad, j * LANES : (j + 1) * LANES
                ]
                total = term if total is None else total + term
            blocks.append(total)
        return split(jnp.concatenate(blocks, axis=0))

    chunks = [tuple(range(f, min(f + 2, fields))) for f in range(0, fields, 2)]

    def add_out(chunk, value):
        for i, f in enumerate(chunk):
            out_ref[f] = out_ref[f] + value[:, i * LANES : (i + 1) * LANES]

    def side_by_side(pairs):
        return (
            jnp.concatenate([p[0] for p in pairs], axis=1),
            jnp.concatenate([p[1] for p in pairs], axis=1),
        )

    def cols(chunk):
        return slice(chunk[0] * LANES, (chunk[-1] + 1) * LANES)

    def out_copy(ex, which, target, region, lane):
        return pltpu.make_async_remote_copy(
            src_ref=send.at[ex, which],
            dst_ref=recv.at[ex, region, sub],
            send_sem=send_sem.at[ex, region, lane],
            recv_sem=recv_sem.at[ex, region, sub],
            device_id=target,
            device_id_type=pl.DeviceIdType.MESH,
        )

    def exchange_copies(ex):
        inner = [out_copy(ex, 0, {"dom": dom, "sub": sibling}, 0, 0)]
        for k in range(1, chips):
            target = {"dom": dom, "sub": 2 * lax.rem(chip + k, chips) + core}
            inner.append(out_copy(ex, 0, target, 0, k))
        lower = [
            out_copy(ex, 1, {"dom": dom - 1, "sub": 2 * c + core}, 2, c) for c in range(chips)
        ]
        upper = [
            out_copy(ex, 1, {"dom": dom + 1, "sub": 2 * c + core}, 1, c) for c in range(chips)
        ]
        return inner, lower, upper

    def arrival(ex, region, s):
        return pltpu.make_async_remote_copy(
            src_ref=send.at[ex, 0],
            dst_ref=recv.at[ex, region, s],
            send_sem=send_sem.at[ex, region, 0],
            recv_sem=recv_sem.at[ex, region, s],
            device_id={"dom": dom, "sub": sub},
            device_id_type=pl.DeviceIdType.MESH,
        )

    def forward(ex, region, s):
        return pltpu.make_async_remote_copy(
            src_ref=recv.at[ex, region, s],
            dst_ref=recv.at[ex, region, s],
            send_sem=forward_sem.at[ex, region, s],
            recv_sem=recv_sem.at[ex, region, s],
            device_id={"dom": dom, "sub": sibling},
            device_id_type=pl.DeviceIdType.MESH,
        )

    def each_region(do, side):
        for k in range(1, chips):
            do(0, 2 * lax.rem(chip + k, chips) + side)

        @pl.when(has_low)
        def _():
            for c in range(chips):
                do(1, 2 * c + side)

        @pl.when(has_high)
        def _():
            for c in range(chips):
                do(2, 2 * c + side)

    is_fast = lax.broadcasted_iota(jnp.int32, (1, LANES), 1) < count_ref[0]

    def stage(ex, carry):
        for f in range(fields):
            at = slice(f * LANES, (f + 1) * LANES)
            start = out_ref[f]
            cur[:, at] = start
            part[:, at] = start
            acc[:, at] = start

        def order(k, weights):
            weight, power = weights
            for chunk in chunks:
                hi, lo = side_by_side([star_rows(cur, f) for f in chunk])
                nxt[:, cols(chunk)] = dot3(pred_w[...], hi, lo, modes)
            weight = weight / (k.astype(F32) + 2.0)
            power = power * 2.0
            value = nxt[...]
            cur[...] = value
            part[...] = part[...] + weight * value
            acc[...] = acc[...] + ((power - 1.0) * weight) * value
            return weight, power

        lax.fori_loop(0, DEGREE, order, (jnp.float32(1.0), jnp.float32(2.0)))
        keep = jnp.logical_or(is_fast, ex == 0)
        for g in range(fields):
            at = slice(g * LANES, (g + 1) * LANES)
            part[:, at] = jnp.where(keep, part[:, at], slow[:, at])
        slow[...] = acc[...]

        for chunk in chunks:
            hi, lo = split(part[:, cols(chunk)])
            value = dot3(proj_w[...], hi, lo, face_rows)
            for i, g in enumerate(chunk):
                for j in range(faces):
                    trace[g * face_pad : (g + 1) * face_pad, j * LANES : (j + 1) * LANES] = value[
                        j * face_pad : (j + 1) * face_pad, i * LANES : (i + 1) * LANES
                    ]

        table = stacked(trace[...])
        rows = trace.shape[0]
        picked = dot(table, hot_send[...])
        picked = picked[:rows] + picked[rows:]
        section = lax.broadcasted_iota(jnp.int32, (fold_rows, LANES), 1) // slots
        for i in range(2):
            lanes = slice(i * LANES, (i + 1) * LANES)
            packed = picked[:fold_rows, lanes]
            for a in range(1, fold):
                packed = jnp.where(
                    section == a, picked[a * fold_rows : (a + 1) * fold_rows, lanes], packed
                )
            send[ex, i] = packed
            if i == 0:
                recv[ex, 0, sub] = packed

        @pl.when(ex == 0)
        def _():
            pl.semaphore_wait(
                barrier, chips * (1 + has_low.astype(jnp.int32) + has_high.astype(jnp.int32))
            )

        inner, lower, upper = exchange_copies(ex)

        @pl.when(has_low)
        def _():
            for copy in lower:
                copy.start()

        @pl.when(has_high)
        def _():
            for copy in upper:
                copy.start()

        for copy in inner:
            copy.start()

        @pl.when(ex == 0)
        def _():
            prepare_update()

        found = dot(table, hot_local[...])
        near[...] = found[:rows] + found[rows:]
        base = vol_rows + face_rows
        for chunk in chunks:
            pairs = []
            for f in chunk:
                vol, own = star_rows(part, f), flux_rows(0, trace, f)
                pairs.append([jnp.concatenate([vol[i], own[i]], axis=0) for i in range(2)])
            hi, lo = side_by_side(pairs)
            add_out(chunk, dot3(upd_w[:, :base], hi, lo, modes))

        def pass_on(region, s):
            arrival(ex, region, s).wait_recv()
            forward(ex, region, s).start()

        each_region(pass_on, core)
        arrival(ex, 0, sibling).wait_recv()
        each_region(lambda region, s: arrival(ex, region, s).wait_recv(), 1 - core)

        for region in range(3):
            for b in range(n_sub // fold):
                blocks = [recv[ex, region, b * fold + i] for i in range(fold)]
                for a in range(fold):
                    value = None
                    for i in range(fold):
                        moved = blocks[i]
                        if i != a:
                            moved = pltpu.roll(moved, ((i - a) * slots) % LANES, 1)
                        value = moved if value is None else jnp.where(section == i, moved, value)
                    first = region * group + b * LANES
                    remote[a * fold_rows : (a + 1) * fold_rows, first : first + LANES] = value
        found = dot(stacked(remote[...]), hot_remote[...])
        near[...] = near[...] + found[:rows] + found[rows:]

        masks = [mask[o].astype(BF16) for o in range(3)]
        for chunk in chunks:
            pairs = []
            for f in chunk:
                hi, lo = flux_rows(1, near, f)
                pairs.append(
                    [
                        jnp.concatenate([value * masks[o] for o in range(3)], axis=0)
                        for value in (hi, lo)
                    ]
                )
            hi, lo = side_by_side(pairs)
            add_out(chunk, dot3(upd_w[:, base:], hi, lo, modes))

        for copy in inner:
            copy.wait_send()

        @pl.when(has_low)
        def _():
            for copy in lower:
                copy.wait_send()

        @pl.when(has_high)
        def _():
            for copy in upper:
                copy.wait_send()

        each_region(lambda region, s: forward(ex, region, s).wait_send(), core)
        return carry

    lax.fori_loop(0, 2, stage, 0)


def local(
    n_dom,
    n_sub,
    modal_state,
    star_mats,
    face_flux,
    stiffness,
    stiff_vol,
    face_proj,
    face_lifting_matrix,
    orient_maps,
    neighbours,
    face_orient,
    send_slots,
    fast_count,
):
    modes, fields, elems = modal_state.shape
    face_modes = orient_maps.shape[1]
    slots = send_slots.shape[1]
    fold = LANES // slots
    face_pad, mode_pad = up(face_modes, 8), up(modes, 16)
    table_rows = up(fields * face_pad, 8 * fold)
    group = n_sub * slots
    width = fields * elems
    upd_cols = 3 * mode_pad + 4 * 4 * face_pad
    any_space = pl.BlockSpec(memory_space=pl.ANY)
    vmem = pl.BlockSpec(memory_space=pltpu.VMEM)
    out = pl.pallas_call(
        functools.partial(kernel, (n_dom, n_sub, modes, fields, face_pad, slots)),
        out_shape=jax.ShapeDtypeStruct((fields, modes, elems), F32),
        in_specs=[any_space] * 8 + [vmem] * 3 + [pl.BlockSpec(memory_space=pltpu.SMEM)],
        out_specs=vmem,
        scratch_shapes=[
            pltpu.VMEM((fields, fields, 3, elems), F32),
            pltpu.VMEM((2, fields, fields, 4, elems), F32),
            pltpu.VMEM((3, modes, modes), F32),
            pltpu.VMEM((3, modes, modes), F32),
            pltpu.VMEM((face_modes, 4, modes), F32),
            pltpu.VMEM((face_modes, 4, modes), F32),
            pltpu.VMEM((3, face_modes, face_modes), F32),
            pltpu.SemaphoreType.DMA((8,)),
            pltpu.VMEM((modes, width), F32),
            pltpu.VMEM((modes, width), F32),
            pltpu.VMEM((modes, width), F32),
            pltpu.VMEM((modes, width), F32),
            pltpu.VMEM((modes, width), F32),
            pltpu.VMEM((table_rows, 4 * elems), F32),
            pltpu.VMEM((table_rows, 4 * elems), F32),
            pltpu.VMEM((table_rows, 3 * group), F32),
            pltpu.VMEM((2 * mode_pad, 3 * mode_pad), BF16),
            pltpu.VMEM((8 * face_pad, modes), BF16),
            pltpu.VMEM((2 * mode_pad, upd_cols), BF16),
            pltpu.VMEM((4 * elems, 4 * elems), BF16),
            pltpu.VMEM((3 * group, 4 * elems), BF16),
            pltpu.VMEM((4 * elems, 2 * LANES), BF16),
            pltpu.VMEM((3, 4 * face_pad, LANES), F32),
            pltpu.VMEM((2, 2, table_rows // fold, LANES), F32),
            pltpu.VMEM((2, 3, n_sub, table_rows // fold, LANES), F32),
            pltpu.SemaphoreType.DMA((2, 3, n_sub)),
            pltpu.SemaphoreType.DMA((2, 3, n_sub)),
            pltpu.SemaphoreType.DMA((2, 3, n_sub)),
        ],
        compiler_params=pltpu.CompilerParams(collective_id=0, has_side_effects=True),
    )(
        modal_state.transpose(1, 0, 2),
        star_mats.transpose(1, 2, 0, 3),
        face_flux.transpose(0, 2, 3, 1, 4),
        stiffness,
        stiff_vol,
        face_proj.transpose(2, 0, 1),
        face_lifting_matrix.transpose(1, 0, 2),
        orient_maps,
        neighbours,
        face_orient,
        send_slots,
        fast_count,
    )
    return out.transpose(1, 0, 2)


def solution(mesh):
    split_last = ("dom", "sub")
    placed = (
        P(None, None, split_last),
        P(None, None, None, split_last),
        P(None, None, None, None, split_last),
        P(),
        P(),
        P(),
        P(),
        P(),
        P(None, split_last),
        P(None, split_last),
        P(None, split_last),
        P(split_last),
    )
    return jax.shard_map(
        functools.partial(local, mesh.shape["dom"], mesh.shape["sub"]),
        mesh=mesh,
        in_specs=placed,
        out_specs=P(None, None, split_last),
        check_vma=False,
    )
```

```python
import functools

import jax
import jax.numpy as jnp
from jax import lax
from jax.experimental import pallas as pl
from jax.experimental.pallas import tpu as pltpu
from jax.sharding import PartitionSpec as P

DEGREE = 5
LANES = 128
F32 = jnp.float32
BF16 = jnp.bfloat16


def up(value, multiple):
    return -(-value // multiple) * multiple


def split(x):
    hi = x.astype(BF16)
    return hi, (x - hi.astype(F32)).astype(BF16)


def stacked(x):
    hi, lo = split(x)
    return jnp.concatenate([hi, lo], axis=0)


def dot(a, b):
    return jnp.dot(a, b, preferred_element_type=F32)


def dot3(w_stack, z_hi, z_lo, rows):
    both = dot(w_stack, z_hi)
    half = w_stack.shape[0] // 2
    return both[:rows] + both[half : half + rows] + dot(w_stack[:half], z_lo)[:rows]


def grow8(x):
    return jnp.concatenate([x, jnp.zeros((8 - x.shape[0], x.shape[1]), F32)], axis=0)


def row_of(ref, *lead_and_row):
    lead, row = lead_and_row[:-1], lead_and_row[-1]
    return ref[(*lead, pl.ds(row, 1), slice(None))]


def kernel(
    sizes,
    state_hbm,
    star_hbm,
    flux_hbm,
    stiff_hbm,
    vol_hbm,
    proj_hbm,
    lift_hbm,
    maps_hbm,
    near_idx_ref,
    orient_ref,
    slots_ref,
    count_ref,
    out_ref,
    star_ref,
    flux_ref,
    stiff_ref,
    vol_ref,
    proj_ref,
    lift_ref,
    maps_ref,
    load_sem,
    cur,
    nxt,
    part,
    slow,
    acc,
    trace,
    near,
    remote,
    pred_w,
    proj_w,
    upd_w,
    hot_local,
    hot_remote,
    hot_send,
    mask,
    send,
    recv,
    send_sem,
    recv_sem,
    forward_sem,
):
    n_dom, n_sub, modes, fields, face_pad, slots = sizes
    width = fields * LANES
    mode_pad = up(modes, 16)
    fold = LANES // slots
    fold_rows = trace.shape[0] // fold
    group = n_sub * slots
    faces = 4
    vol_rows, face_rows = 3 * mode_pad, faces * face_pad
    loads = [
        pltpu.make_async_copy(source, target, load_sem.at[i])
        for i, (source, target) in enumerate(
            [
                (stiff_hbm, stiff_ref),
                (vol_hbm, vol_ref),
                (proj_hbm, proj_ref),
                (lift_hbm, lift_ref),
                (maps_hbm, maps_ref),
                (state_hbm, out_ref),
                (star_hbm, star_ref),
                (flux_hbm, flux_ref),
            ]
        )
    ]
    for load in loads:
        load.start()
    dom, sub = lax.axis_index("dom"), lax.axis_index("sub")
    has_low, has_high = dom > 0, dom < n_dom - 1

    barrier = pltpu.get_barrier_semaphore()

    def greet(d, s):
        pl.semaphore_signal(
            barrier, inc=1, device_id={"dom": d, "sub": s}, device_id_type=pl.DeviceIdType.MESH
        )

    chips = n_sub // 2
    chip, core = sub // 2, lax.rem(sub, 2)
    sibling = 2 * chip + 1 - core

    greet(dom, sibling)
    for k in range(1, chips):
        greet(dom, 2 * lax.rem(chip + k, chips) + core)

    @pl.when(has_low)
    def _():
        for c in range(chips):
            greet(dom - 1, 2 * c + core)

    @pl.when(has_high)
    def _():
        for c in range(chips):
            greet(dom + 1, 2 * c + core)

    @pl.when(jnp.logical_not(has_low))
    def _():
        recv[:, 1] = jnp.zeros((2, *recv.shape[2:]), F32)

    @pl.when(jnp.logical_not(has_high))
    def _():
        recv[:, 2] = jnp.zeros((2, *recv.shape[2:]), F32)

    trace[fields * face_pad :, :] = jnp.zeros(
        (trace.shape[0] - fields * face_pad, trace.shape[1]), F32
    )
    slow[...] = jnp.zeros_like(slow)

    def one_hot(row, rows):
        at = lax.broadcasted_iota(jnp.int32, (rows, LANES), 0)
        return jnp.where(at == row, 1.0, 0.0).astype(BF16)

    own_count = faces * LANES
    def at_columns(rows, columns, test):
        row = lax.broadcasted_iota(jnp.int32, (rows, columns), 0)
        column = lax.broadcasted_iota(jnp.int32, (rows, columns), 1)
        return jnp.where(test(row, column), 1.0, 0.0).astype(BF16)

    tiled = dot(
        stacked(grow8(slots_ref[...].astype(F32))),
        at_columns(slots, LANES, lambda row, column: column % slots == row),
    )
    tiled = (tiled[:8] + tiled[8:]).astype(jnp.int32)
    for i in range(2):
        hot_send[:, i * LANES : (i + 1) * LANES] = one_hot(tiled[i : i + 1, :], own_count)

    for load in loads[:5]:
        load.wait()

    def grow(x, rows):
        return jnp.concatenate([x, jnp.zeros((rows - x.shape[0], x.shape[1]), F32)], axis=0)

    def shifted(rows, columns, shift):
        return at_columns(rows, columns, lambda row, column: column == row + shift)

    def spread(ref):
        value = None
        for d in range(3):
            term = dot(stacked(grow(ref[d], mode_pad)), shifted(modes, vol_rows, d * mode_pad))
            value = term if value is None else value + term
        return value

    face_modes = maps_ref.shape[1]
    pred_w[...] = (-spread(stiff_ref)).astype(BF16)
    def by_face(ref):
        return jnp.concatenate([grow(ref[:, j, :], face_pad) for j in range(faces)], axis=0)

    proj_w[...] = stacked(by_face(proj_ref))
    def prepare_update():
        for j in range(faces):
            row = near_idx_ref[j : j + 1, :]
            hot_local[:, j * LANES : (j + 1) * LANES] = one_hot(row, own_count)
            hot_remote[:, j * LANES : (j + 1) * LANES] = one_hot(row - own_count, 3 * group)
            turn = orient_ref[j : j + 1, :]
            for o in range(3):
                mask[o, j * face_pad : (j + 1) * face_pad, :] = jnp.broadcast_to(
                    jnp.where(turn == o, 1.0, 0.0), (face_pad, LANES)
                )
        upd_w[:, :vol_rows] = spread(vol_ref).astype(BF16)
        same = shifted(mode_pad, modes, 0)
        turn_lift = []
        for value in split(-by_face(lift_ref)):
            turn_lift.append(
                lax.dot_general(same, value, (((1,), (1,)), ((), ())), preferred_element_type=F32)
            )
        turn_lift = jnp.concatenate(turn_lift, axis=0).astype(BF16)
        upd_w[:, vol_rows : vol_rows + face_rows] = turn_lift
        turned = None
        for o in range(3):
            place = at_columns(
                face_modes,
                3 * face_rows,
                lambda row, column: (column // face_rows == o) & (column % face_pad == row),
            )
            both = dot(stacked(grow(maps_ref[o], up(face_pad, 16))), place)
            term = both[:face_pad] + both[up(face_pad, 16) :][:face_pad]
            turned = term if turned is None else turned + term
        turned = jnp.concatenate([turned] * faces, axis=0)
        row = lax.broadcasted_iota(jnp.int32, turned.shape, 0)
        column = lax.broadcasted_iota(jnp.int32, turned.shape, 1)
        turned = jnp.where(column % face_rows // face_pad == row // face_pad, turned, 0.0)
        upd_w[:, vol_rows + face_rows :] = stacked(dot3(turn_lift, *split(turned), mode_pad))

    for load in loads[5:]:
        load.wait()

    def star_rows(src, f):
        high, low = [], []
        for d in range(3):
            for start in range(0, modes, 16):
                count = min(16, modes - start)
                total = None
                for g in range(fields):
                    term = row_of(star_ref, f, g, d) * src[
                        start : start + count, g * LANES : (g + 1) * LANES
                    ]
                    total = term if total is None else total + term
                if count < 16:
                    total = jnp.concatenate([total, jnp.zeros((16 - count, LANES), F32)], axis=0)
                hi, lo = split(total)
                high.append(hi)
                low.append(lo)
        return jnp.concatenate(high, axis=0), jnp.concatenate(low, axis=0)

    def flux_rows(side, src, f):
        blocks = []
        for j in range(faces):
            total = None
            for g in range(fields):
                term = row_of(flux_ref, side, f, g, j) * src[
                    g * face_pad : (g + 1) * face_pad, j * LANES : (j + 1) * LANES
                ]
                total = term if total is None else total + term
            blocks.append(total)
        return split(jnp.concatenate(blocks, axis=0))

    chunks = [tuple(range(f, min(f + 2, fields))) for f in range(0, fields, 2)]

    def add_out(chunk, value):
        for i, f in enumerate(chunk):
            out_ref[f] = out_ref[f] + value[:, i * LANES : (i + 1) * LANES]

    def side_by_side(pairs):
        return (
            jnp.concatenate([p[0] for p in pairs], axis=1),
            jnp.concatenate([p[1] for p in pairs], axis=1),
        )

    def cols(chunk):
        return slice(chunk[0] * LANES, (chunk[-1] + 1) * LANES)

    def out_copy(ex, which, target, region, lane):
        return pltpu.make_async_remote_copy(
            src_ref=send.at[ex, which],
            dst_ref=recv.at[ex, region, sub],
            send_sem=send_sem.at[ex, region, lane],
            recv_sem=recv_sem.at[ex, region, sub],
            device_id=target,
            device_id_type=pl.DeviceIdType.MESH,
        )

    def exchange_copies(ex):
        inner = [out_copy(ex, 0, {"dom": dom, "sub": sibling}, 0, 0)]
        for k in range(1, chips):
            target = {"dom": dom, "sub": 2 * lax.rem(chip + k, chips) + core}
            inner.append(out_copy(ex, 0, target, 0, k))
        lower = [
            out_copy(ex, 1, {"dom": dom - 1, "sub": 2 * c + core}, 2, c) for c in range(chips)
        ]
        upper = [
            out_copy(ex, 1, {"dom": dom + 1, "sub": 2 * c + core}, 1, c) for c in range(chips)
        ]
        return inner, lower, upper

    def arrival(ex, region, s):
        return pltpu.make_async_remote_copy(
            src_ref=send.at[ex, 0],
            dst_ref=recv.at[ex, region, s],
            send_sem=send_sem.at[ex, region, 0],
            recv_sem=recv_sem.at[ex, region, s],
            device_id={"dom": dom, "sub": sub},
            device_id_type=pl.DeviceIdType.MESH,
        )

    def forward(ex, region, s):
        return pltpu.make_async_remote_copy(
            src_ref=recv.at[ex, region, s],
            dst_ref=recv.at[ex, region, s],
            send_sem=forward_sem.at[ex, region, s],
            recv_sem=recv_sem.at[ex, region, s],
            device_id={"dom": dom, "sub": sibling},
            device_id_type=pl.DeviceIdType.MESH,
        )

    def each_region(do, side):
        @pl.when(has_low)
        def _():
            for c in range(chips):
                do(1, 2 * c + side)

        @pl.when(has_high)
        def _():
            for c in range(chips):
                do(2, 2 * c + side)

        for k in range(1, chips):
            do(0, 2 * lax.rem(chip + k, chips) + side)

    is_fast = lax.broadcasted_iota(jnp.int32, (1, LANES), 1) < count_ref[0]

    def stage(ex, carry):
        for f in range(fields):
            at = slice(f * LANES, (f + 1) * LANES)
            start = out_ref[f]
            cur[:, at] = start
            part[:, at] = start
            acc[:, at] = start

        def order(k, weights):
            weight, power = weights
            for chunk in chunks:
                hi, lo = side_by_side([star_rows(cur, f) for f in chunk])
                nxt[:, cols(chunk)] = dot3(pred_w[...], hi, lo, modes)
            weight = weight / (k.astype(F32) + 2.0)
            power = power * 2.0
            value = nxt[...]
            cur[...] = value
            part[...] = part[...] + weight * value
            acc[...] = acc[...] + ((power - 1.0) * weight) * value
            return weight, power

        lax.fori_loop(0, DEGREE, order, (jnp.float32(1.0), jnp.float32(2.0)))
        keep = jnp.logical_or(is_fast, ex == 0)
        for g in range(fields):
            at = slice(g * LANES, (g + 1) * LANES)
            part[:, at] = jnp.where(keep, part[:, at], slow[:, at])
        slow[...] = acc[...]

        for chunk in chunks:
            hi, lo = split(part[:, cols(chunk)])
            value = dot3(proj_w[...], hi, lo, face_rows)
            for i, g in enumerate(chunk):
                for j in range(faces):
                    trace[g * face_pad : (g + 1) * face_pad, j * LANES : (j + 1) * LANES] = value[
                        j * face_pad : (j + 1) * face_pad, i * LANES : (i + 1) * LANES
                    ]

        table = stacked(trace[...])
        rows = trace.shape[0]
        picked = dot(table, hot_send[...])
        picked = picked[:rows] + picked[rows:]
        section = lax.broadcasted_iota(jnp.int32, (fold_rows, LANES), 1) // slots
        for i in range(2):
            lanes = slice(i * LANES, (i + 1) * LANES)
            packed = picked[:fold_rows, lanes]
            for a in range(1, fold):
                packed = jnp.where(
                    section == a, picked[a * fold_rows : (a + 1) * fold_rows, lanes], packed
                )
            send[ex, i] = packed
            if i == 0:
                recv[ex, 0, sub] = packed

        @pl.when(ex == 0)
        def _():
            pl.semaphore_wait(
                barrier, chips * (1 + has_low.astype(jnp.int32) + has_high.astype(jnp.int32))
            )

        inner, lower, upper = exchange_copies(ex)

        @pl.when(has_low)
        def _():
            for copy in lower:
                copy.start()

        @pl.when(has_high)
        def _():
            for copy in upper:
                copy.start()

        for copy in inner:
            copy.start()

        @pl.when(ex == 0)
        def _():
            prepare_update()

        found = dot(table, hot_local[...])
        near[...] = found[:rows] + found[rows:]
        base = vol_rows + face_rows
        for chunk in chunks:
            pairs = []
            for f in chunk:
                vol, own = star_rows(part, f), flux_rows(0, trace, f)
                pairs.append([jnp.concatenate([vol[i], own[i]], axis=0) for i in range(2)])
            hi, lo = side_by_side(pairs)
            add_out(chunk, dot3(upd_w[:, :base], hi, lo, modes))

        def pass_on(region, s):
            arrival(ex, region, s).wait_recv()
            forward(ex, region, s).start()

        each_region(pass_on, core)
        arrival(ex, 0, sibling).wait_recv()
        each_region(lambda region, s: arrival(ex, region, s).wait_recv(), 1 - core)

        for region in range(3):
            for b in range(n_sub // fold):
                blocks = [recv[ex, region, b * fold + i] for i in range(fold)]
                for a in range(fold):
                    value = None
                    for i in range(fold):
                        moved = blocks[i]
                        if i != a:
                            moved = pltpu.roll(moved, ((i - a) * slots) % LANES, 1)
                        value = moved if value is None else jnp.where(section == i, moved, value)
                    first = region * group + b * LANES
                    remote[a * fold_rows : (a + 1) * fold_rows, first : first + LANES] = value
        found = dot(stacked(remote[...]), hot_remote[...])
        near[...] = near[...] + found[:rows] + found[rows:]

        masks = [mask[o].astype(BF16) for o in range(3)]
        for chunk in chunks:
            pairs = []
            for f in chunk:
                hi, lo = flux_rows(1, near, f)
                pairs.append(
                    [
                        jnp.concatenate([value * masks[o] for o in range(3)], axis=0)
                        for value in (hi, lo)
                    ]
                )
            hi, lo = side_by_side(pairs)
            add_out(chunk, dot3(upd_w[:, base:], hi, lo, modes))

        for copy in inner:
            copy.wait_send()

        @pl.when(has_low)
        def _():
            for copy in lower:
                copy.wait_send()

        @pl.when(has_high)
        def _():
            for copy in upper:
                copy.wait_send()

        each_region(lambda region, s: forward(ex, region, s).wait_send(), core)
        return carry

    lax.fori_loop(0, 2, stage, 0)


def local(
    n_dom,
    n_sub,
    modal_state,
    star_mats,
    face_flux,
    stiffness,
    stiff_vol,
    face_proj,
    face_lifting_matrix,
    orient_maps,
    neighbours,
    face_orient,
    send_slots,
    fast_count,
):
    modes, fields, elems = modal_state.shape
    face_modes = orient_maps.shape[1]
    slots = send_slots.shape[1]
    fold = LANES // slots
    face_pad, mode_pad = up(face_modes, 8), up(modes, 16)
    table_rows = up(fields * face_pad, 8 * fold)
    group = n_sub * slots
    width = fields * elems
    upd_cols = 3 * mode_pad + 4 * 4 * face_pad
    any_space = pl.BlockSpec(memory_space=pl.ANY)
    vmem = pl.BlockSpec(memory_space=pltpu.VMEM)
    out = pl.pallas_call(
        functools.partial(kernel, (n_dom, n_sub, modes, fields, face_pad, slots)),
        out_shape=jax.ShapeDtypeStruct((fields, modes, elems), F32),
        in_specs=[any_space] * 8 + [vmem] * 3 + [pl.BlockSpec(memory_space=pltpu.SMEM)],
        out_specs=vmem,
        scratch_shapes=[
            pltpu.VMEM((fields, fields, 3, elems), F32),
            pltpu.VMEM((2, fields, fields, 4, elems), F32),
            pltpu.VMEM((3, modes, modes), F32),
            pltpu.VMEM((3, modes, modes), F32),
            pltpu.VMEM((face_modes, 4, modes), F32),
            pltpu.VMEM((face_modes, 4, modes), F32),
            pltpu.VMEM((3, face_modes, face_modes), F32),
            pltpu.SemaphoreType.DMA((8,)),
            pltpu.VMEM((modes, width), F32),
            pltpu.VMEM((modes, width), F32),
            pltpu.VMEM((modes, width), F32),
            pltpu.VMEM((modes, width), F32),
            pltpu.VMEM((modes, width), F32),
            pltpu.VMEM((table_rows, 4 * elems), F32),
            pltpu.VMEM((table_rows, 4 * elems), F32),
            pltpu.VMEM((table_rows, 3 * group), F32),
            pltpu.VMEM((2 * mode_pad, 3 * mode_pad), BF16),
            pltpu.VMEM((8 * face_pad, modes), BF16),
            pltpu.VMEM((2 * mode_pad, upd_cols), BF16),
            pltpu.VMEM((4 * elems, 4 * elems), BF16),
            pltpu.VMEM((3 * group, 4 * elems), BF16),
            pltpu.VMEM((4 * elems, 2 * LANES), BF16),
            pltpu.VMEM((3, 4 * face_pad, LANES), F32),
            pltpu.VMEM((2, 2, table_rows // fold, LANES), F32),
            pltpu.VMEM((2, 3, n_sub, table_rows // fold, LANES), F32),
            pltpu.SemaphoreType.DMA((2, 3, n_sub)),
            pltpu.SemaphoreType.DMA((2, 3, n_sub)),
            pltpu.SemaphoreType.DMA((2, 3, n_sub)),
        ],
        compiler_params=pltpu.CompilerParams(collective_id=0, has_side_effects=True),
    )(
        modal_state.transpose(1, 0, 2),
        star_mats.transpose(1, 2, 0, 3),
        face_flux.transpose(0, 2, 3, 1, 4),
        stiffness,
        stiff_vol,
        face_proj.transpose(2, 0, 1),
        face_lifting_matrix.transpose(1, 0, 2),
        orient_maps,
        neighbours,
        face_orient,
        send_slots,
        fast_count,
    )
    return out.transpose(1, 0, 2)


def solution(mesh):
    split_last = ("dom", "sub")
    placed = (
        P(None, None, split_last),
        P(None, None, None, split_last),
        P(None, None, None, None, split_last),
        P(),
        P(),
        P(),
        P(),
        P(),
        P(None, split_last),
        P(None, split_last),
        P(None, split_last),
        P(split_last),
    )
    return jax.shard_map(
        functools.partial(local, mesh.shape["dom"], mesh.shape["sub"]),
        mesh=mesh,
        in_specs=placed,
        out_specs=P(None, None, split_last),
        check_vma=False,
    )
```
